128 devices in a mesh: ctx: 16 (over y, x), wa: 8 (over z, core).
Axes of the slice: x: 4, y: 4, z: 4, core: 2. Of those that a mesh axis runs over, the one named last changes fastest.
Arguments:
- tokens: bfloat16 [4096, 1024], P('ctx'), may hold values from -6 to 6
- segment_ids: int32 [4096], replicated, may hold values from 0 to 3, as said below
- positions: int32 [4096], P('ctx'), may hold values from 0 to 2558, as said below
- mixnorm_gain: float32 [1024], replicated, may hold values from 0.5 to 1.5
- bgate_weight: bfloat16 [1024, 1024], P(None, 'wa'), may hold values from -0.1875 to 0.1875
- cgate_weight: bfloat16 [1024, 1024], P(None, 'wa'), may hold values from -0.1875 to 0.1875
- xvalue_weight: bfloat16 [1024, 1024], P(None, 'wa'), may hold values from -0.1875 to 0.1875
- conv_kernel: float32 [3, 1024], P(None, 'wa'), may hold values from -4 to 4
- mixout_weight: bfloat16 [1024, 1024], P(None, 'wa'), may hold values from -0.1875 to 0.1875
- lowernorm_gain: float32 [1024], replicated, may hold values from 0.5 to 1.5
- lowergate_weight: bfloat16 [1024, 4608], P(None, 'wa'), may hold values from -0.1875 to 0.1875
- lowerlift_weight: bfloat16 [1024, 4608], P(None, 'wa'), may hold values from -0.1875 to 0.1875
- lowerdown_weight: bfloat16 [1024, 4608], P(None, 'wa'), may hold values from -0.09375 to 0.09375
- attnnorm_gain: float32 [1024], replicated, may hold values from 0.5 to 1.5
- query_weight: bfloat16 [1024, 1024], P(None, 'wa'), may hold values from -0.1875 to 0.1875
- key_weight: bfloat16 [1024, 512], P(None, 'wa'), may hold values from -0.1875 to 0.1875
- value_weight: bfloat16 [1024, 512], P(None, 'wa'), may hold values from -0.1875 to 0.1875
- querynorm_gain: float32 [64], replicated, may hold values from 1.2 to 3
- keynorm_gain: float32 [64], replicated, may hold values from 1.2 to 3
- attnout_weight: bfloat16 [1024, 1024], P(None, 'wa'), may hold values from -0.75 to 0.75
- uppernorm_gain: float32 [1024], replicated, may hold values from 0.5 to 1.5
- uppergate_weight: bfloat16 [1024, 4608], P(None, 'wa'), may hold values from -0.1875 to 0.1875
- upperlift_weight: bfloat16 [1024, 4608], P(None, 'wa'), may hold values from -0.1875 to 0.1875
- upperdown_weight: bfloat16 [1024, 4608], P(None, 'wa'), may hold values from -0.09375 to 0.09375
- cotangent: bfloat16 [4096, 1024], P('ctx'), may hold values from -6 to 6
Outputs:
- block_output: bfloat16 [4096, 1024], P('ctx')
- tokens_grad: float32 [4096, 1024], P('ctx')
- mixnorm_grad: float32 [1024], P('ctx')
- bgate_grad: float32 [1024, 1024], P('ctx', 'wa')
- cgate_grad: float32 [1024, 1024], P('ctx', 'wa')
- xvalue_grad: float32 [1024, 1024], P('ctx', 'wa')
- kernel_grad: float32 [3, 1024], P(None, 'wa')
- mixout_grad: float32 [1024, 1024], P('ctx', 'wa')
- lowernorm_grad: float32 [1024], P('ctx')
- lowergate_grad: float32 [1024, 4608], P('ctx', 'wa')
- lowerlift_grad: float32 [1024, 4608], P('ctx', 'wa')
- lowerdown_grad: float32 [1024, 4608], P('ctx', 'wa')
- attnnorm_grad: float32 [1024], P('ctx')
- query_grad: float32 [1024, 1024], P('ctx', 'wa')
- key_grad: float32 [1024, 512], P('ctx', 'wa')
- value_grad: float32 [1024, 512], P('ctx', 'wa')
- querynorm_grad: float32 [64], replicated
- keynorm_grad: float32 [64], replicated
- attnout_grad: float32 [1024, 1024], P('ctx', 'wa')
- uppernorm_grad: float32 [1024], P('ctx')
- uppergate_grad: float32 [1024, 4608], P('ctx', 'wa')
- upperlift_grad: float32 [1024, 4608], P('ctx', 'wa')
- upperdown_grad: float32 [1024, 4608], P('ctx', 'wa')
The draws below stay inside these ranges and needn't reach their ends.
Inputs may be any that keep to these rules, and one draw needn't show every extreme that they name: `segment_ids`: segment ids never fall from one token to the next; there are 4 documents of one token or more, and the longest has exactly 2048 tokens. Within a document the positions rise by one from token to token; each document starts below 512, the longest document starts at 511, and some document starts at 0.
All inputs are finite; a program needn't handle non-finite values.
Results may differ from the reference program's by a relative error of at most 0.028.
The reference program's roundings to bfloat16 on the way count: a program that leaves them out, or rounds other values in their place, can miss the bound.
Values may be sent and summed in bfloat16 or wider, within the bound.
No kernel may reach another device: no remote copies, remote signals or barrier semaphores. Data moves between devices by JAX's collectives and lax.ppermute only.
A program may use at most 128 MiB of HBM per device.

```python
import math
import jax
import jax.numpy as jnp
from jax import lax

D = 1024
FF = 4608
H = 16
KV = 8
HD = 64
DOCS = 4
POS_START = 512
TOKENS = 4096


def document_layout(key):
    base_key = jax.random.fold_in(key, 17)
    cut_key, slot_key, shift_key = jax.random.split(base_key, 3)
    longest = TOKENS // 2
    cut_points = jnp.sort(jax.random.permutation(cut_key, longest - 1)[:DOCS - 2] + 1).astype(jnp.int32)
    bounds = jnp.concatenate([jnp.zeros((1,), jnp.int32), cut_points, jnp.full((1,), longest, jnp.int32)])
    shorter = bounds[1:] - bounds[:-1]
    slot_index = jax.random.randint(slot_key, (), 0, DOCS)
    doc_order = jnp.arange(DOCS, dtype=jnp.int32)
    source_index = jnp.clip(doc_order - (doc_order > slot_index).astype(jnp.int32), 0, DOCS - 2)
    lengths = jnp.where(doc_order == slot_index, longest, shorter[source_index]).astype(jnp.int32)
    starts = jnp.cumsum(lengths) - lengths
    token_index = jnp.arange(TOKENS, dtype=jnp.int32)
    segment = jnp.sum((token_index[:, None] >= starts[None, 1:]).astype(jnp.int32), axis=1)
    drawn_offsets = jax.random.randint(shift_key, (DOCS,), 0, POS_START)
    zero_slot = (slot_index + 1) % DOCS
    offsets = jnp.where(doc_order == slot_index, POS_START - 1, jnp.where(doc_order == zero_slot, 0, drawn_offsets)).astype(jnp.int32)
    position_ids = token_index - starts[segment] + offsets[segment]
    return (segment.astype(jnp.int32), position_ids.astype(jnp.int32))


def draw_segment_ids(key, part):
    return document_layout(key)[0]


def draw_positions(key, part):
    return document_layout(key)[1]


def norm_gain_draw(local_key):
    return jnp.exp(jax.random.uniform(local_key, (HD,), jnp.float32, math.log(1.2), math.log(2.4)))


def draw_querynorm_gain(key, part):
    return norm_gain_draw(jax.random.fold_in(key, 31))


def draw_keynorm_gain(key, part):
    return norm_gain_draw(jax.random.fold_in(key, 37))


def steps_of(own_key, dims, pieces, least, largest):
    def one(dim, parts):
        heights = jax.random.uniform(jax.random.fold_in(jax.random.fold_in(own_key, 6), dim), (parts,), jnp.float32, least / len(pieces), largest / len(pieces))
        return jnp.repeat(jnp.exp(heights), dims[dim] // parts).reshape((-1,) + (1,) * (len(dims) - dim - 1))

    loudness = one(*pieces[0])
    for cut in pieces[1:]:
        loudness = loudness * one(*cut)
    return loudness


def noise(key, extent, width, most, pieces=(), kind=jnp.bfloat16):
    array = width * jax.random.normal(key, extent, jnp.float32)
    if pieces:
        array = array * steps_of(key, extent, pieces, -0.22, 0.18)
    return jnp.clip(array, -most, most).astype(kind)


def setup_inputs(seed: int = 0) -> dict:
    seeds = jax.random.split(jax.random.key(seed), 26)
    return {
        "tokens": noise(seeds[0], (TOKENS, D), 1.0, 6.0, ((0, 16),)),
        "segment_ids": draw_segment_ids(jax.random.fold_in(seeds[25], 71), 0),
        "positions": draw_positions(jax.random.fold_in(seeds[25], 71), 0),
        "mixnorm_gain": jnp.clip(1.0 + 0.1 * jax.random.normal(seeds[3], (D,), jnp.float32), 0.5, 1.5),
        "bgate_weight": noise(seeds[4], (D, D), D ** -0.5, 0.1875, ((1, 8),)),
        "cgate_weight": noise(seeds[5], (D, D), D ** -0.5, 0.1875, ((1, 8),)),
        "xvalue_weight": noise(seeds[6], (D, D), D ** -0.5, 0.1875, ((1, 8),)),
        "conv_kernel": noise(seeds[7], (3, D), 1.0, 4.0, ((1, 8),), jnp.float32),
        "mixout_weight": noise(seeds[8], (D, D), D ** -0.5, 0.1875, ((1, 8),)),
        "lowernorm_gain": jnp.clip(1.0 + 0.1 * jax.random.normal(seeds[9], (D,), jnp.float32), 0.5, 1.5),
        "lowergate_weight": noise(seeds[10], (D, FF), D ** -0.5, 0.1875, ((1, 8),)),
        "lowerlift_weight": noise(seeds[11], (D, FF), D ** -0.5, 0.1875, ((1, 8),)),
        "lowerdown_weight": noise(seeds[12], (D, FF), FF ** -0.5, 0.09375, ((1, 8),)),
        "attnnorm_gain": jnp.clip(1.0 + 0.1 * jax.random.normal(seeds[13], (D,), jnp.float32), 0.5, 1.5),
        "query_weight": noise(seeds[14], (D, H * HD), D ** -0.5, 0.1875, ((1, 8),)),
        "key_weight": noise(seeds[15], (D, KV * HD), D ** -0.5, 0.1875, ((1, 8),)),
        "value_weight": noise(seeds[16], (D, KV * HD), D ** -0.5, 0.1875, ((1, 8),)),
        "querynorm_gain": draw_querynorm_gain(jax.random.fold_in(seeds[25], 71), 0),
        "keynorm_gain": draw_keynorm_gain(jax.random.fold_in(seeds[25], 71), 0),
        "attnout_weight": noise(seeds[19], (D, H * HD), HD ** -0.5, 0.75, ((1, 8),)),
        "uppernorm_gain": jnp.clip(1.0 + 0.1 * jax.random.normal(seeds[20], (D,), jnp.float32), 0.5, 1.5),
        "uppergate_weight": noise(seeds[21], (D, FF), D ** -0.5, 0.1875, ((1, 8),)),
        "upperlift_weight": noise(seeds[22], (D, FF), D ** -0.5, 0.1875, ((1, 8),)),
        "upperdown_weight": noise(seeds[23], (D, FF), FF ** -0.5, 0.09375, ((1, 8),)),
        "cotangent": noise(seeds[24], (TOKENS, D), 1.0, 6.0, ((0, 16),)),
    }


EPS = 1e-05
ROPE_BASE = 1000000.0
NEG_BIG = -1e+30

def round_trip(values):
    return lax.optimization_barrier(values.astype(jnp.bfloat16)).astype(jnp.float32)

def norm_forward(hidden, gain_vec):
    inverse = lax.rsqrt(lax.optimization_barrier(jnp.mean(hidden * hidden, axis=-1, keepdims=True)) + EPS)
    unit_rows = hidden * inverse
    return (unit_rows * gain_vec, unit_rows, inverse)

def norm_backward(grad_out, unit_rows, inverse, gain_vec):
    scaled = grad_out * gain_vec
    return inverse * (scaled - unit_rows * lax.optimization_barrier(jnp.mean(scaled * unit_rows, axis=-1, keepdims=True)))

def gain_total(grad_out, unit_rows):
    return lax.optimization_barrier(jnp.sum((grad_out * unit_rows).reshape(-1, grad_out.shape[-1]), axis=0))

def rope_tables(positions, head_dim):
    half_dim = head_dim // 2
    frequency = jnp.power(jnp.float32(ROPE_BASE), -2.0 * jnp.arange(half_dim, dtype=jnp.float32) / head_dim)
    angles = positions.astype(jnp.float32)[:, None] * frequency[None, :]
    return (jnp.cos(angles), jnp.sin(angles))

def rotate(vectors, cosine_table, sine_table):
    half_dim = vectors.shape[-1] // 2
    front_half = vectors[..., :half_dim]
    back_half = vectors[..., half_dim:]
    cosine_wide = cosine_table[:, None, None, :]
    sine_wide = sine_table[:, None, None, :]
    return jnp.concatenate([front_half * cosine_wide - back_half * sine_wide, back_half * cosine_wide + front_half * sine_wide], axis=-1)

def rotate_back(grads, cosine_table, sine_table):
    half_dim = grads.shape[-1] // 2
    front_half = grads[..., :half_dim]
    back_half = grads[..., half_dim:]
    cosine_wide = cosine_table[:, None, None, :]
    sine_wide = sine_table[:, None, None, :]
    return jnp.concatenate([front_half * cosine_wide + back_half * sine_wide, back_half * cosine_wide - front_half * sine_wide], axis=-1)

def contract_rows(left_side, right_side):
    return jnp.dot(left_side.T, right_side, preferred_element_type=jnp.float32)

def times_transposed(left_side, right_side):
    return jnp.dot(left_side, right_side.T, preferred_element_type=jnp.float32)

def ffn_forward(hidden, gain_vec, gate_weight, lift_weight, down_weight):
    normed, unit_rows, inverse = norm_forward(hidden, gain_vec)
    normed_rounded = normed.astype(jnp.bfloat16)
    gate_values = jnp.dot(normed_rounded, gate_weight, preferred_element_type=jnp.float32)
    lift_values = jnp.dot(normed_rounded, lift_weight, preferred_element_type=jnp.float32)
    sigmoid_values = jax.nn.sigmoid(gate_values)
    activation = (gate_values * sigmoid_values * lift_values).astype(jnp.bfloat16)
    result = hidden + times_transposed(activation, down_weight)
    return (result, (normed_rounded, unit_rows, inverse, gate_values, lift_values, sigmoid_values, activation))

def ffn_backward(grad_hidden, saved, gain_vec, gate_weight, lift_weight, down_weight):
    normed_rounded, unit_rows, inverse, gate_values, lift_values, sigmoid_values, activation = saved
    grad_rounded = grad_hidden.astype(jnp.bfloat16)
    grad_activation = jnp.dot(grad_rounded, down_weight, preferred_element_type=jnp.float32)
    down_grad = contract_rows(grad_rounded, activation)
    grad_gate = (grad_activation * lift_values * sigmoid_values * (1.0 + gate_values * (1.0 - sigmoid_values))).astype(jnp.bfloat16)
    grad_lift = (grad_activation * gate_values * sigmoid_values).astype(jnp.bfloat16)
    gate_grad = contract_rows(normed_rounded, grad_gate)
    lift_grad = contract_rows(normed_rounded, grad_lift)
    grad_normed = times_transposed(grad_gate, gate_weight) + times_transposed(grad_lift, lift_weight)
    gain_grad = gain_total(grad_normed, unit_rows)
    grad_input = grad_hidden + norm_backward(grad_normed, unit_rows, inverse, gain_vec)
    return (grad_input, (gain_grad, gate_grad, lift_grad, down_grad))

def visible_block(first_row, block_rows, segment_ids):
    key_index = jnp.arange(TOKENS, dtype=jnp.int32)
    query_index = first_row + jnp.arange(block_rows, dtype=jnp.int32)
    query_ids = lax.dynamic_slice_in_dim(segment_ids, first_row, block_rows, 0)
    allowed = (key_index[None, :] <= query_index[:, None]) & (segment_ids[None, :] == query_ids[:, None])
    return allowed[:, None, None, :]

def attention_forward(query_rot, key_rot, value_rows, segment_ids):
    block_rows = math.gcd(TOKENS, 512)
    score_scale = HD ** (-0.5)

    def one_block(block_id):
        first_row = block_id * block_rows
        query_rows = lax.dynamic_slice_in_dim(query_rot, first_row, block_rows, 0)
        visible = visible_block(first_row, block_rows, segment_ids)
        scores = jnp.einsum('tkgd,skd->tkgs', query_rows, key_rot) * score_scale
        scores = jnp.where(visible, scores, NEG_BIG)
        top_score = lax.optimization_barrier(jnp.max(scores, axis=-1))
        weights = jnp.where(visible, jnp.exp(scores - top_score[..., None]), 0.0)
        total_weight = lax.optimization_barrier(jnp.sum(weights, axis=-1))
        accumulated = jnp.einsum('tkgs,skd->tkgd', round_trip(weights), value_rows)
        return (accumulated / total_weight[..., None], top_score + jnp.log(total_weight))
    block_ids = jnp.arange(TOKENS // block_rows, dtype=jnp.int32)
    mixed_heads, log_total = lax.map(one_block, block_ids)
    return (mixed_heads.reshape(TOKENS, KV, H // KV, HD), log_total.reshape(TOKENS, KV, H // KV))

def attention_backward(query_rot, key_rot, value_rows, segment_ids, log_total, grad_heads, delta_rows):
    block_rows = math.gcd(TOKENS, 512)
    score_scale = HD ** (-0.5)

    def one_block(running, block_id):
        keys_back, values_back = running
        first_row = block_id * block_rows
        query_rows = lax.dynamic_slice_in_dim(query_rot, first_row, block_rows, 0)
        grad_rows = lax.dynamic_slice_in_dim(grad_heads, first_row, block_rows, 0)
        total_rows = lax.dynamic_slice_in_dim(log_total, first_row, block_rows, 0)
        delta_block = lax.dynamic_slice_in_dim(delta_rows, first_row, block_rows, 0)
        visible = visible_block(first_row, block_rows, segment_ids)
        scores = jnp.einsum('tkgd,skd->tkgs', query_rows, key_rot) * score_scale
        scores = jnp.where(visible, scores, NEG_BIG)
        weights = jnp.where(visible, jnp.exp(scores - total_rows[..., None]), 0.0)
        grad_weights = jnp.einsum('tkgd,skd->tkgs', grad_rows, value_rows)
        grad_scores = round_trip(weights * (grad_weights - delta_block[..., None]))
        query_part = jnp.einsum('tkgs,skd->tkgd', grad_scores, key_rot) * score_scale
        keys_back = keys_back + jnp.einsum('tkgs,tkgd->skd', grad_scores, query_rows) * score_scale
        values_back = values_back + jnp.einsum('tkgs,tkgd->skd', round_trip(weights), grad_rows)
        return ((keys_back, values_back), query_part)
    empty = jnp.zeros((TOKENS, KV, HD), jnp.float32)
    block_ids = jnp.arange(TOKENS // block_rows, dtype=jnp.int32)
    (keys_back, values_back), query_back = lax.scan(one_block, (empty, empty), block_ids)
    return (query_back.reshape(TOKENS, KV, H // KV, HD), keys_back, values_back)

def reference(tokens, segment_ids, positions, mixnorm_gain, bgate_weight, cgate_weight, xvalue_weight, conv_kernel, mixout_weight, lowernorm_gain, lowergate_weight, lowerlift_weight, lowerdown_weight, attnnorm_gain, query_weight, key_weight, value_weight, querynorm_gain, keynorm_gain, attnout_weight, uppernorm_gain, uppergate_weight, upperlift_weight, upperdown_weight, cotangent):
    group_size = H // KV
    edge_ids = jnp.full((2,), -1, jnp.int32)
    padded_ids = jnp.concatenate([edge_ids, segment_ids.astype(jnp.int32), edge_ids])
    own_ids = padded_ids[2:TOKENS + 2]
    back_one = (padded_ids[1:TOKENS + 1] == own_ids)[:, None]
    back_two = (padded_ids[0:TOKENS] == own_ids)[:, None]
    ahead_one = (padded_ids[3:TOKENS + 3] == own_ids)[:, None]
    ahead_two = (padded_ids[4:TOKENS + 4] == own_ids)[:, None]
    base_hidden = tokens.astype(jnp.float32)
    mixer_normed, mixer_unit, mixer_inverse = norm_forward(base_hidden, mixnorm_gain)
    mixer_rounded = mixer_normed.astype(jnp.bfloat16)
    gate_before = jnp.dot(mixer_rounded, bgate_weight, preferred_element_type=jnp.float32)
    gate_after = jnp.dot(mixer_rounded, cgate_weight, preferred_element_type=jnp.float32)
    conv_value = jnp.dot(mixer_rounded, xvalue_weight, preferred_element_type=jnp.float32)
    conv_input = (gate_before * conv_value).astype(jnp.bfloat16)
    extended = jnp.concatenate([jnp.zeros((2, D), jnp.bfloat16), conv_input], axis=0).astype(jnp.float32)
    conv_result = conv_kernel[0] * extended[2:] + conv_kernel[1] * jnp.where(back_one, extended[1:TOKENS + 1], 0.0) + conv_kernel[2] * jnp.where(back_two, extended[0:TOKENS], 0.0)
    gated_rounded = (gate_after * conv_result).astype(jnp.bfloat16)
    after_mixer = base_hidden + times_transposed(gated_rounded, mixout_weight)
    after_lower, lower_saved = ffn_forward(after_mixer, lowernorm_gain, lowergate_weight, lowerlift_weight, lowerdown_weight)
    attention_normed, attention_unit, attention_inverse = norm_forward(after_lower, attnnorm_gain)
    attention_rounded = attention_normed.astype(jnp.bfloat16)
    query_raw = jnp.dot(attention_rounded, query_weight, preferred_element_type=jnp.float32).reshape(TOKENS, KV, group_size, HD)
    keys_raw = jnp.dot(attention_rounded, key_weight, preferred_element_type=jnp.float32).reshape(TOKENS, KV, 1, HD)
    value_rows = round_trip(jnp.dot(attention_rounded, value_weight, preferred_element_type=jnp.float32)).reshape(TOKENS, KV, HD)
    query_normed, query_unit, query_inverse = norm_forward(query_raw, querynorm_gain)
    keys_normed, keys_unit, keys_inverse = norm_forward(keys_raw, keynorm_gain)
    cosine_table, sine_table = rope_tables(positions, HD)
    query_rotated = round_trip(rotate(query_normed, cosine_table, sine_table))
    keys_rotated = round_trip(rotate(keys_normed, cosine_table, sine_table)).reshape(TOKENS, KV, HD)
    mixed_heads, log_total = attention_forward(query_rotated, keys_rotated, value_rows, segment_ids)
    mixed_rounded = mixed_heads.astype(jnp.bfloat16).reshape(TOKENS, H * HD)
    after_attention = after_lower + times_transposed(mixed_rounded, attnout_weight)
    after_upper, upper_saved = ffn_forward(after_attention, uppernorm_gain, uppergate_weight, upperlift_weight, upperdown_weight)
    block_output = after_upper.astype(jnp.bfloat16)
    grad_three, upper_terms = ffn_backward(cotangent.astype(jnp.float32), upper_saved, uppernorm_gain, uppergate_weight, upperlift_weight, upperdown_weight)
    three_rounded = grad_three.astype(jnp.bfloat16)
    grad_mixed = jnp.dot(three_rounded, attnout_weight, preferred_element_type=jnp.float32)
    attnout_grad = contract_rows(three_rounded, mixed_rounded)
    grad_heads = round_trip(grad_mixed).reshape(TOKENS, KV, group_size, HD)
    delta_rows = lax.optimization_barrier(jnp.sum(grad_heads * mixed_heads, axis=-1))
    query_back, keys_back, values_back = attention_backward(query_rotated, keys_rotated, value_rows, segment_ids, log_total, grad_heads, delta_rows)
    query_upstream = rotate_back(query_back, cosine_table, sine_table)
    keys_upstream = rotate_back(keys_back.reshape(TOKENS, KV, 1, HD), cosine_table, sine_table)
    querynorm_grad = gain_total(query_upstream, query_unit)
    keynorm_grad = gain_total(keys_upstream, keys_unit)
    grad_query = norm_backward(query_upstream, query_unit, query_inverse, querynorm_gain).astype(jnp.bfloat16).reshape(TOKENS, H * HD)
    grad_keys = norm_backward(keys_upstream, keys_unit, keys_inverse, keynorm_gain).astype(jnp.bfloat16).reshape(TOKENS, KV * HD)
    grad_values = values_back.astype(jnp.bfloat16).reshape(TOKENS, KV * HD)
    query_grad = contract_rows(attention_rounded, grad_query)
    key_grad = contract_rows(attention_rounded, grad_keys)
    value_grad = contract_rows(attention_rounded, grad_values)
    grad_attention = times_transposed(grad_query, query_weight) + times_transposed(grad_keys, key_weight) + times_transposed(grad_values, value_weight)
    attnnorm_grad = gain_total(grad_attention, attention_unit)
    grad_two = grad_three + norm_backward(grad_attention, attention_unit, attention_inverse, attnnorm_gain)
    grad_one, lower_terms = ffn_backward(grad_two, lower_saved, lowernorm_gain, lowergate_weight, lowerlift_weight, lowerdown_weight)
    one_rounded = grad_one.astype(jnp.bfloat16)
    grad_gated = jnp.dot(one_rounded, mixout_weight, preferred_element_type=jnp.float32)
    mixout_grad = contract_rows(one_rounded, gated_rounded)
    grad_after_gate = (grad_gated * conv_result).astype(jnp.bfloat16)
    grad_conv = grad_gated * gate_after
    grad_extended = jnp.concatenate([grad_conv, jnp.zeros((2, D), jnp.float32)], axis=0)
    grad_conv_input = conv_kernel[0] * grad_conv + conv_kernel[1] * jnp.where(ahead_one, grad_extended[1:TOKENS + 1], 0.0) + conv_kernel[2] * jnp.where(ahead_two, grad_extended[2:TOKENS + 2], 0.0)
    kernel_grad = jnp.stack([lax.optimization_barrier(jnp.sum(grad_conv * extended[2:], axis=0)), lax.optimization_barrier(jnp.sum(grad_conv * jnp.where(back_one, extended[1:TOKENS + 1], 0.0), axis=0)), lax.optimization_barrier(jnp.sum(grad_conv * jnp.where(back_two, extended[0:TOKENS], 0.0), axis=0))])
    grad_before = (grad_conv_input * conv_value).astype(jnp.bfloat16)
    grad_value = (grad_conv_input * gate_before).astype(jnp.bfloat16)
    bgate_grad = contract_rows(mixer_rounded, grad_before)
    cgate_grad = contract_rows(mixer_rounded, grad_after_gate)
    xvalue_grad = contract_rows(mixer_rounded, grad_value)
    grad_mixer = times_transposed(grad_before, bgate_weight) + times_transposed(grad_after_gate, cgate_weight) + times_transposed(grad_value, xvalue_weight)
    mixnorm_grad = gain_total(grad_mixer, mixer_unit)
    tokens_grad = grad_one + norm_backward(grad_mixer, mixer_unit, mixer_inverse, mixnorm_gain)
    return (block_output, tokens_grad, mixnorm_grad, bgate_grad, cgate_grad, xvalue_grad, kernel_grad, mixout_grad, lower_terms[0], lower_terms[1], lower_terms[2], lower_terms[3], attnnorm_grad, query_grad, key_grad, value_grad, querynorm_grad, keynorm_grad, attnout_grad, upper_terms[0], upper_terms[1], upper_terms[2], upper_terms[3])
```

```python
import jax
import jax.numpy as jnp
from jax import lax
from jax.sharding import PartitionSpec as P

EPS = 1e-05
ROPE_BASE = 1000000.0
NEG_BIG = -1e30


CORES = 2
CHIPS = 4
REACH = 2048


def passed_along(value, axis, steps):
    count = lax.axis_size(axis)
    initial, last = (max(0, -steps), min(count, count - steps))
    return lax.ppermute(value, axis, [(source, source + steps) for source in range(initial, last)])


def to_partner(value):
    return lax.ppermute(value, "wa", [(w, w ^ 1) for w in range(CORES * CHIPS)])


def along_z(value, steps):
    return lax.ppermute(
        value,
        "wa",
        [
            (CORES * z + c, CORES * ((z + steps) % CHIPS) + c)
            for z in range(CHIPS)
            for c in range(CORES)
        ],
    )


def rolled(value, shift, axis):
    return lax.dynamic_slice_in_dim(
        jnp.concatenate([value, value], axis=axis), shift, value.shape[axis], axis
    )


def norm_forward(hidden, gain_vec):
    inverse = lax.rsqrt(jnp.mean(hidden * hidden, axis=-1, keepdims=True) + EPS)
    unit_rows = hidden * inverse
    return (unit_rows * gain_vec, unit_rows, inverse)


def norm_backward(grad_out, unit_rows, inverse, gain_vec):
    scaled = grad_out * gain_vec
    return inverse * (scaled - unit_rows * jnp.mean(scaled * unit_rows, axis=-1, keepdims=True))


def gain_total(grad_out, unit_rows):
    return jnp.sum((grad_out * unit_rows).reshape(-1, grad_out.shape[-1]), axis=0)


def rope_tables(positions, head_dim):
    half_dim = head_dim // 2
    frequency = jnp.power(
        jnp.float32(ROPE_BASE), -2.0 * jnp.arange(half_dim, dtype=jnp.float32) / head_dim
    )
    angles = positions.astype(jnp.float32)[:, None] * frequency[None, :]
    return (jnp.cos(angles), jnp.sin(angles))


def rotate(vectors, cosine_table, sine_table):
    half_dim = vectors.shape[-1] // 2
    front_half = vectors[..., :half_dim]
    back_half = vectors[..., half_dim:]
    cosine_wide = cosine_table[:, None, None, :]
    sine_wide = sine_table[:, None, None, :]
    return jnp.concatenate(
        [
            front_half * cosine_wide - back_half * sine_wide,
            back_half * cosine_wide + front_half * sine_wide,
        ],
        axis=-1,
    )


def rotate_back(grads, cosine_table, sine_table):
    half_dim = grads.shape[-1] // 2
    front_half = grads[..., :half_dim]
    back_half = grads[..., half_dim:]
    cosine_wide = cosine_table[:, None, None, :]
    sine_wide = sine_table[:, None, None, :]
    return jnp.concatenate(
        [
            front_half * cosine_wide + back_half * sine_wide,
            back_half * cosine_wide - front_half * sine_wide,
        ],
        axis=-1,
    )


def contract_rows(left_side, right_side):
    return lax.dot_general(
        left_side, right_side, (((0,), (0,)), ((), ())), preferred_element_type=jnp.float32
    )


def times_transposed(left_side, right_side):
    return lax.dot_general(
        left_side, right_side, (((1,), (1,)), ((), ())), preferred_element_type=jnp.float32
    )


def shards(
    tokens,
    segment_ids,
    positions,
    mixnorm_gain,
    bgate_weight,
    cgate_weight,
    xvalue_weight,
    conv_kernel,
    mixout_weight,
    lowernorm_gain,
    lowergate_weight,
    lowerlift_weight,
    lowerdown_weight,
    attnnorm_gain,
    query_weight,
    key_weight,
    value_weight,
    querynorm_gain,
    keynorm_gain,
    attnout_weight,
    uppernorm_gain,
    uppergate_weight,
    upperlift_weight,
    upperdown_weight,
    cotangent,
):
    row_count = tokens.shape[0]
    model_width = tokens.shape[1]
    head_dim = querynorm_gain.shape[0]
    group_size = query_weight.shape[1] // key_weight.shape[1]
    score_scale = head_dim ** (-0.5)
    block_count = lax.axis_size("ctx")
    gain_width = model_width // block_count
    block_index = lax.axis_index("ctx")
    first_row = block_index * row_count
    wa_index = lax.axis_index("wa")
    core = wa_index % CORES
    chip = wa_index // CORES
    half = row_count // CORES
    share = half // CHIPS
    own_start = core * half + chip * share
    reach_blocks = REACH // row_count
    bf16 = jnp.bfloat16

    def to_own_order(values):
        parts = values.reshape((CORES, CHIPS, share) + values.shape[1:])
        parts = rolled(rolled(parts, core, 0), chip, 1)
        return parts.reshape(values.shape)

    def to_token_order(values):
        parts = values.reshape((CORES, CHIPS, share) + values.shape[1:])
        parts = rolled(rolled(parts, (CORES - core) % CORES, 0), (CHIPS - chip) % CHIPS, 1)
        return parts.reshape(values.shape)

    def own_rows(values):
        return lax.dynamic_slice_in_dim(values, own_start, share, 0)

    def sum_own(partial):
        arrived = to_partner(partial[half:].astype(bf16))
        kept = partial[:half] + arrived.astype(jnp.float32)
        pieces = [
            along_z(kept[b * share : (b + 1) * share].astype(bf16), b) for b in range(1, CHIPS)
        ]
        total = kept[:share]
        for piece in pieces:
            total = total + piece.astype(jnp.float32)
        return total

    def sum_token_order(partial):
        sent = lax.dynamic_slice_in_dim(partial, (1 - core) * half, half, 0).astype(bf16)
        arrived = to_partner(sent)
        kept = lax.dynamic_slice_in_dim(partial, core * half, half, 0) + arrived.astype(jnp.float32)

        def piece_of(steps):
            return lax.dynamic_slice_in_dim(kept, ((chip + steps) % CHIPS) * share, share, 0)

        pieces = [along_z(piece_of(b).astype(bf16), b) for b in range(1, CHIPS)]
        total = piece_of(0)
        for piece in pieces:
            total = total + piece.astype(jnp.float32)
        return total

    def all_rows(owned):
        pieces = [owned] + [along_z(owned, CHIPS - b) for b in range(1, CHIPS)]
        mine = jnp.concatenate(pieces, axis=0)
        return jnp.concatenate([mine, to_partner(mine)], axis=0)

    def ffn_forward(hidden, gain_vec, gate_weight, lift_weight):
        normed, unit_rows, inverse = norm_forward(hidden, gain_vec)
        normed_rounded = all_rows(normed.astype(bf16))
        gate_values = jnp.dot(normed_rounded, gate_weight, preferred_element_type=jnp.float32)
        lift_values = jnp.dot(normed_rounded, lift_weight, preferred_element_type=jnp.float32)
        sigmoid_values = jax.nn.sigmoid(gate_values)
        activation = (gate_values * sigmoid_values * lift_values).astype(bf16)
        return (
            activation,
            (
                normed_rounded,
                unit_rows,
                inverse,
                gate_values,
                lift_values,
                sigmoid_values,
                activation,
            ),
        )

    def ffn_backward(
        grad_hidden, grad_rounded, saved, gain_vec, gate_weight, lift_weight, down_weight
    ):
        normed_rounded, unit_rows, inverse, gate_values, lift_values, sigmoid_values, activation = (
            saved
        )
        grad_activation = jnp.dot(grad_rounded, down_weight, preferred_element_type=jnp.float32)
        grad_gate = (
            grad_activation
            * lift_values
            * sigmoid_values
            * (1.0 + gate_values * (1.0 - sigmoid_values))
        ).astype(bf16)
        grad_lift = (grad_activation * gate_values * sigmoid_values).astype(bf16)
        grad_normed = sum_own(
            times_transposed(grad_gate, gate_weight) + times_transposed(grad_lift, lift_weight)
        )
        gate_grad = contract_rows(normed_rounded, grad_gate)
        lift_grad = contract_rows(normed_rounded, grad_lift)
        down_grad = contract_rows(grad_rounded, activation)
        gain_part = gain_total(grad_normed, unit_rows)
        grad_input = grad_hidden + norm_backward(grad_normed, unit_rows, inverse, gain_vec)
        return (grad_input, (gain_part, gate_grad, lift_grad, down_grad))

    edge_ids = jnp.full((2,), -1, jnp.int32)
    padded_ids = jnp.concatenate([edge_ids, segment_ids, edge_ids])
    window_ids = lax.dynamic_slice_in_dim(padded_ids, first_row, row_count + 4)
    own_ids = window_ids[2 : row_count + 2]
    back_one = (window_ids[1 : row_count + 1] == own_ids)[:, None]
    back_two = (window_ids[0:row_count] == own_ids)[:, None]
    ahead_one = (window_ids[3 : row_count + 3] == own_ids)[:, None]
    ahead_two = (window_ids[4 : row_count + 4] == own_ids)[:, None]

    base_hidden = tokens.astype(jnp.float32)
    mixer_normed, mixer_unit, mixer_inverse = norm_forward(base_hidden, mixnorm_gain)
    mixer_rounded = mixer_normed.astype(bf16)
    gate_before = jnp.dot(mixer_rounded, bgate_weight, preferred_element_type=jnp.float32)
    conv_value = jnp.dot(mixer_rounded, xvalue_weight, preferred_element_type=jnp.float32)
    conv_input = (gate_before * conv_value).astype(bf16)
    carried = passed_along(conv_input[row_count - 2 :], "ctx", 1)
    gate_after = jnp.dot(mixer_rounded, cgate_weight, preferred_element_type=jnp.float32)
    extended = jnp.concatenate([carried, conv_input], axis=0).astype(jnp.float32)
    conv_result = (
        conv_kernel[0] * extended[2:]
        + conv_kernel[1] * jnp.where(back_one, extended[1 : row_count + 1], 0.0)
        + conv_kernel[2] * jnp.where(back_two, extended[0:row_count], 0.0)
    )
    gated_rounded = (gate_after * conv_result).astype(bf16)
    own_tokens = own_rows(tokens).astype(jnp.float32)
    after_mixer = own_tokens + sum_token_order(times_transposed(gated_rounded, mixout_weight))

    lower_activation, lower_saved = ffn_forward(
        after_mixer, lowernorm_gain, lowergate_weight, lowerlift_weight
    )
    after_lower = after_mixer + sum_own(times_transposed(lower_activation, lowerdown_weight))

    attention_normed, attention_unit, attention_inverse = norm_forward(after_lower, attnnorm_gain)
    attention_rounded = all_rows(attention_normed.astype(bf16))
    query_raw = jnp.dot(
        attention_rounded, query_weight, preferred_element_type=jnp.float32
    ).reshape(row_count, 1, group_size, head_dim)
    keys_raw = jnp.dot(attention_rounded, key_weight, preferred_element_type=jnp.float32).reshape(
        row_count, 1, 1, head_dim
    )
    value_rows = jnp.dot(
        attention_rounded, value_weight, preferred_element_type=jnp.float32
    ).astype(bf16)
    query_normed, query_unit, query_inverse = norm_forward(query_raw, querynorm_gain)
    keys_normed, keys_unit, keys_inverse = norm_forward(keys_raw, keynorm_gain)
    cosine_table, sine_table = rope_tables(to_own_order(positions), head_dim)
    query_rotated = rotate(query_normed, cosine_table, sine_table).astype(bf16)
    keys_rotated = (
        rotate(keys_normed, cosine_table, sine_table).astype(bf16).reshape(row_count, head_dim)
    )

    own_pairs = jnp.concatenate([keys_rotated, value_rows], axis=1)
    arrived_pairs = lax.all_to_all(
        jnp.broadcast_to(own_pairs[None], (block_count,) + own_pairs.shape),
        "ctx",
        0,
        0,
        tiled=True,
    )
    pairs = lax.dynamic_slice_in_dim(
        jnp.concatenate(
            [jnp.zeros((reach_blocks,) + own_pairs.shape, bf16), arrived_pairs], axis=0
        ),
        block_index,
        reach_blocks + 1,
        0,
    ).reshape(-1, 2 * head_dim)
    key_heads = pairs[:, :head_dim]
    value_heads = pairs[:, head_dim:]
    block_starts = (
        first_row + row_count * (jnp.arange(reach_blocks + 1, dtype=jnp.int32) - reach_blocks)
    )
    id_window = lax.dynamic_slice_in_dim(
        jnp.concatenate([jnp.full((reach_blocks * row_count,), -1, jnp.int32), segment_ids]),
        first_row,
        (reach_blocks + 1) * row_count,
    ).reshape(reach_blocks + 1, row_count)
    row_order = to_own_order(jnp.arange(row_count, dtype=jnp.int32))
    query_index = first_row + row_order
    query_ids = to_own_order(own_ids)
    key_index = (block_starts[:, None] + row_order[None, :]).reshape(-1)
    key_ids = jax.vmap(to_own_order)(id_window).reshape(-1)
    allowed = (key_index[None, :] <= query_index[:, None]) & (key_ids[None, :] == query_ids[:, None])
    visible = allowed[:, None, :]
    query_heads = query_rotated.reshape(row_count, group_size, head_dim)
    scores = (
        jnp.einsum("tgd,sd->tgs", query_heads, key_heads, preferred_element_type=jnp.float32)
        * score_scale
    )
    scores = jnp.where(visible, scores, NEG_BIG)
    top_score = jnp.max(scores, axis=-1)
    weights = jnp.where(visible, jnp.exp(scores - top_score[..., None]), 0.0)
    total_weight = jnp.sum(weights, axis=-1)
    accumulated = jnp.einsum(
        "tgs,sd->tgd", weights.astype(bf16), value_heads, preferred_element_type=jnp.float32
    )
    mixed_heads = accumulated / total_weight[..., None]
    log_total = top_score + jnp.log(total_weight)
    mixed_rounded = mixed_heads.astype(bf16).reshape(row_count, group_size * head_dim)
    after_attention = after_lower + sum_own(times_transposed(mixed_rounded, attnout_weight))

    upper_activation, upper_saved = ffn_forward(
        after_attention, uppernorm_gain, uppergate_weight, upperlift_weight
    )
    own_order_cotangent = to_own_order(cotangent)
    grad_three, upper_terms = ffn_backward(
        own_rows(cotangent).astype(jnp.float32),
        own_order_cotangent,
        upper_saved,
        uppernorm_gain,
        uppergate_weight,
        upperlift_weight,
        upperdown_weight,
    )
    after_upper = after_attention + sum_own(times_transposed(upper_activation, upperdown_weight))
    block_output = to_token_order(all_rows(after_upper.astype(bf16)))

    three_rounded = all_rows(grad_three.astype(bf16))
    grad_mixed = jnp.dot(three_rounded, attnout_weight, preferred_element_type=jnp.float32)
    grad_heads = grad_mixed.astype(bf16).reshape(row_count, group_size, head_dim)
    delta_rows = jnp.sum(grad_heads.astype(jnp.float32) * mixed_heads, axis=-1)
    weights = jnp.where(visible, jnp.exp(scores - log_total[..., None]), 0.0)
    grad_weights = jnp.einsum(
        "tgd,sd->tgs", grad_heads, value_heads, preferred_element_type=jnp.float32
    )
    grad_scores = (weights * (grad_weights - delta_rows[..., None])).astype(bf16)
    query_back = (
        jnp.einsum("tgs,sd->tgd", grad_scores, key_heads, preferred_element_type=jnp.float32)
        * score_scale
    )
    key_part = (
        jnp.einsum("tgs,tgd->sd", grad_scores, query_heads, preferred_element_type=jnp.float32)
        * score_scale
    )
    value_part = jnp.einsum(
        "tgs,tgd->sd", weights.astype(bf16), grad_heads, preferred_element_type=jnp.float32
    )
    pair_parts = jnp.concatenate([key_part, value_part], axis=1).reshape(
        reach_blocks + 1, row_count, 2 * head_dim
    )
    pairs_back = pair_parts[reach_blocks]
    for k in range(1, reach_blocks + 1):
        pairs_back = pairs_back + passed_along(
            pair_parts[reach_blocks - k].astype(bf16), "ctx", -k
        ).astype(jnp.float32)
    keys_back = pairs_back[:, :head_dim]
    values_back = pairs_back[:, head_dim:]

    query_upstream = rotate_back(
        query_back.reshape(row_count, 1, group_size, head_dim), cosine_table, sine_table
    )
    keys_upstream = rotate_back(
        keys_back.reshape(row_count, 1, 1, head_dim), cosine_table, sine_table
    )
    querynorm_part = gain_total(query_upstream, query_unit)
    keynorm_part = gain_total(keys_upstream, keys_unit)
    grad_query = (
        norm_backward(query_upstream, query_unit, query_inverse, querynorm_gain)
        .astype(bf16)
        .reshape(row_count, group_size * head_dim)
    )
    grad_keys = (
        norm_backward(keys_upstream, keys_unit, keys_inverse, keynorm_gain)
        .astype(bf16)
        .reshape(row_count, head_dim)
    )
    grad_values = values_back.astype(bf16)
    grad_attention = sum_own(
        times_transposed(grad_query, query_weight)
        + times_transposed(grad_keys, key_weight)
        + times_transposed(grad_values, value_weight)
    )
    attnnorm_part = gain_total(grad_attention, attention_unit)
    grad_two = grad_three + norm_backward(
        grad_attention, attention_unit, attention_inverse, attnnorm_gain
    )
    grad_one, lower_terms = ffn_backward(
        grad_two,
        all_rows(grad_two.astype(bf16)),
        lower_saved,
        lowernorm_gain,
        lowergate_weight,
        lowerlift_weight,
        lowerdown_weight,
    )
    attention_grads = [
        contract_rows(attention_rounded, grad_query),
        contract_rows(attention_rounded, grad_keys),
        contract_rows(attention_rounded, grad_values),
        contract_rows(three_rounded, mixed_rounded),
    ]
    one_rounded = to_token_order(all_rows(grad_one.astype(bf16)))
    grad_gated = jnp.dot(one_rounded, mixout_weight, preferred_element_type=jnp.float32)
    grad_conv = grad_gated * gate_after
    following = passed_along(grad_conv[:2], "ctx", -1)
    grad_after_gate = (grad_gated * conv_result).astype(bf16)
    mixout_grad = contract_rows(one_rounded, gated_rounded)
    grad_extended = jnp.concatenate([grad_conv, following], axis=0)
    grad_conv_input = (
        conv_kernel[0] * grad_conv
        + conv_kernel[1] * jnp.where(ahead_one, grad_extended[1 : row_count + 1], 0.0)
        + conv_kernel[2] * jnp.where(ahead_two, grad_extended[2 : row_count + 2], 0.0)
    )
    kernel_local = jnp.stack(
        [
            jnp.sum(grad_conv * extended[2:], axis=0),
            jnp.sum(grad_conv * jnp.where(back_one, extended[1 : row_count + 1], 0.0), axis=0),
            jnp.sum(grad_conv * jnp.where(back_two, extended[0:row_count], 0.0), axis=0),
        ]
    )
    grad_before = (grad_conv_input * conv_value).astype(bf16)
    grad_value = (grad_conv_input * gate_before).astype(bf16)
    mixer_partial = (
        times_transposed(grad_before, bgate_weight)
        + times_transposed(grad_after_gate, cgate_weight)
        + times_transposed(grad_value, xvalue_weight)
    )
    grad_mixer = sum_token_order(mixer_partial)
    mixnorm_part = jnp.sum(mixer_partial * mixer_unit, axis=0)
    own_unit, own_inverse = (own_rows(mixer_unit), own_rows(mixer_inverse))
    own_tokens_grad = grad_one + norm_backward(grad_mixer, own_unit, own_inverse, mixnorm_gain)
    tokens_held = to_token_order(all_rows(own_tokens_grad.astype(bf16))).astype(jnp.float32)

    last_grads = jnp.concatenate(
        [
            contract_rows(mixer_rounded, grad_before),
            contract_rows(mixer_rounded, grad_after_gate),
            contract_rows(mixer_rounded, grad_value),
            mixout_grad,
        ],
        axis=1,
    ).astype(bf16)
    last_width = last_grads.shape[1]

    def by_block(vector):
        return vector.reshape(block_count, gain_width)

    def for_all(vector):
        return jnp.broadcast_to(vector.reshape(1, -1), (block_count, vector.size))

    small_parts = jnp.concatenate(
        [
            for_all(kernel_local),
            by_block(mixnorm_part),
            by_block(lower_terms[0]),
            by_block(attnnorm_part),
            by_block(upper_terms[0]),
            for_all(querynorm_part),
            for_all(keynorm_part),
        ],
        axis=1,
    ).astype(bf16)
    small_width = small_parts.shape[1]
    small_rows = -(-small_width // last_width)
    small_parts = jnp.pad(small_parts, ((0, 0), (0, small_rows * last_width - small_width)))
    outgoing = jnp.concatenate(
        [
            last_grads.reshape(block_count, gain_width, last_width),
            small_parts.reshape(block_count, small_rows, last_width),
        ],
        axis=1,
    )
    incoming = lax.all_to_all(outgoing, "ctx", 0, 0, tiled=True)
    last_sums = jnp.sum(incoming.astype(jnp.float32), axis=0)
    last_shares = last_sums[:gain_width]
    small_sums = last_sums[gain_width:].reshape(-1)[:small_width]
    kernel_grad = small_sums[: kernel_local.size].reshape(kernel_local.shape)
    gain_sums = small_sums[kernel_local.size :]
    gain_sums = gain_sums + to_partner(gain_sums)
    gain_pieces = [along_z(gain_sums, b) for b in range(1, CHIPS)]
    for piece in gain_pieces:
        gain_sums = gain_sums + piece
    gains = gain_sums.reshape(-1, gain_width)
    querynorm_grad = gain_sums[4 * gain_width : 4 * gain_width + head_dim]
    keynorm_grad = gain_sums[4 * gain_width + head_dim :]

    def scattered(parts):
        merged = lax.psum_scatter(
            jnp.concatenate([part.astype(bf16) for part in parts], axis=1),
            "ctx",
            scatter_dimension=0,
            tiled=True,
        ).astype(jnp.float32)
        bounds = [0]
        for part in parts:
            bounds.append(bounds[-1] + part.shape[1])
        return [merged[:, low:high] for low, high in zip(bounds[:-1], bounds[1:])]

    upper_shares = scattered(list(upper_terms[1:]))
    lower_shares = scattered(list(lower_terms[1:]) + attention_grads)
    channels = bgate_weight.shape[1]
    return (
        block_output,
        tokens_held,
        gains[0],
        last_shares[:, :channels],
        last_shares[:, channels : 2 * channels],
        last_shares[:, 2 * channels : 3 * channels],
        kernel_grad,
        last_shares[:, 3 * channels :],
        gains[1],
        lower_shares[0],
        lower_shares[1],
        lower_shares[2],
        gains[2],
        lower_shares[3],
        lower_shares[4],
        lower_shares[5],
        querynorm_grad,
        keynorm_grad,
        lower_shares[6],
        gains[3],
        upper_shares[0],
        upper_shares[1],
        upper_shares[2],
    )


def solution(mesh):
    return jax.shard_map(
        shards,
        mesh=mesh,
        in_specs=(
            P("ctx", None),
            P(),
            P("ctx"),
            P(),
            P(None, "wa"),
            P(None, "wa"),
            P(None, "wa"),
            P(None, "wa"),
            P(None, "wa"),
            P(),
            P(None, "wa"),
            P(None, "wa"),
            P(None, "wa"),
            P(),
            P(None, "wa"),
            P(None, "wa"),
            P(None, "wa"),
            P(),
            P(),
            P(None, "wa"),
            P(),
            P(None, "wa"),
            P(None, "wa"),
            P(None, "wa"),
            P("ctx", None),
        ),
        out_specs=(
            P("ctx", None),
            P("ctx", None),
            P("ctx"),
            P("ctx", "wa"),
            P("ctx", "wa"),
            P("ctx", "wa"),
            P(None, "wa"),
            P("ctx", "wa"),
            P("ctx"),
            P("ctx", "wa"),
            P("ctx", "wa"),
            P("ctx", "wa"),
            P("ctx"),
            P("ctx", "wa"),
            P("ctx", "wa"),
            P("ctx", "wa"),
            P(),
            P(),
            P("ctx", "wa"),
            P("ctx"),
            P("ctx", "wa"),
            P("ctx", "wa"),
            P("ctx", "wa"),
        ),
        check_vma=False,
    )
```

```python
import jax
import jax.numpy as jnp
from jax import lax
from jax.sharding import PartitionSpec as P

EPS = 1e-05
ROPE_BASE = 1000000.0
NEG_BIG = -1e30


CORES = 2
CHIPS = 4
REACH = 2048


def passed_along(value, axis, steps):
    count = lax.axis_size(axis)
    initial, last = (max(0, -steps), min(count, count - steps))
    return lax.ppermute(value, axis, [(source, source + steps) for source in range(initial, last)])


def to_partner(value):
    return lax.ppermute(value, "wa", [(w, w ^ 1) for w in range(CORES * CHIPS)])


def along_z(value, steps):
    return lax.ppermute(
        value,
        "wa",
        [
            (CORES * z + c, CORES * ((z + steps) % CHIPS) + c)
            for z in range(CHIPS)
            for c in range(CORES)
        ],
    )


def rolled(value, shift, axis):
    return lax.dynamic_slice_in_dim(
        jnp.concatenate([value, value], axis=axis), shift, value.shape[axis], axis
    )


def norm_forward(hidden, gain_vec):
    inverse = lax.rsqrt(jnp.mean(hidden * hidden, axis=-1, keepdims=True) + EPS)
    unit_rows = hidden * inverse
    return (unit_rows * gain_vec, unit_rows, inverse)


def norm_backward(grad_out, unit_rows, inverse, gain_vec):
    scaled = grad_out * gain_vec
    return inverse * (scaled - unit_rows * jnp.mean(scaled * unit_rows, axis=-1, keepdims=True))


def gain_total(grad_out, unit_rows):
    return jnp.sum((grad_out * unit_rows).reshape(-1, grad_out.shape[-1]), axis=0)


def rope_tables(positions, head_dim):
    half_dim = head_dim // 2
    frequency = jnp.power(
        jnp.float32(ROPE_BASE), -2.0 * jnp.arange(half_dim, dtype=jnp.float32) / head_dim
    )
    angles = positions.astype(jnp.float32)[:, None] * frequency[None, :]
    return (jnp.cos(angles), jnp.sin(angles))


def rotate(vectors, cosine_table, sine_table):
    half_dim = vectors.shape[-1] // 2
    front_half = vectors[..., :half_dim]
    back_half = vectors[..., half_dim:]
    cosine_wide = cosine_table[:, None, None, :]
    sine_wide = sine_table[:, None, None, :]
    return jnp.concatenate(
        [
            front_half * cosine_wide - back_half * sine_wide,
            back_half * cosine_wide + front_half * sine_wide,
        ],
        axis=-1,
    )


def rotate_back(grads, cosine_table, sine_table):
    half_dim = grads.shape[-1] // 2
    front_half = grads[..., :half_dim]
    back_half = grads[..., half_dim:]
    cosine_wide = cosine_table[:, None, None, :]
    sine_wide = sine_table[:, None, None, :]
    return jnp.concatenate(
        [
            front_half * cosine_wide + back_half * sine_wide,
            back_half * cosine_wide - front_half * sine_wide,
        ],
        axis=-1,
    )


def contract_rows(left_side, right_side):
    return lax.dot_general(
        left_side, right_side, (((0,), (0,)), ((), ())), preferred_element_type=jnp.float32
    )


def times_transposed(left_side, right_side):
    return lax.dot_general(
        left_side, right_side, (((1,), (1,)), ((), ())), preferred_element_type=jnp.float32
    )


def shards(
    tokens,
    segment_ids,
    positions,
    mixnorm_gain,
    bgate_weight,
    cgate_weight,
    xvalue_weight,
    conv_kernel,
    mixout_weight,
    lowernorm_gain,
    lowergate_weight,
    lowerlift_weight,
    lowerdown_weight,
    attnnorm_gain,
    query_weight,
    key_weight,
    value_weight,
    querynorm_gain,
    keynorm_gain,
    attnout_weight,
    uppernorm_gain,
    uppergate_weight,
    upperlift_weight,
    upperdown_weight,
    cotangent,
):
    row_count = tokens.shape[0]
    model_width = tokens.shape[1]
    head_dim = querynorm_gain.shape[0]
    group_size = query_weight.shape[1] // key_weight.shape[1]
    score_scale = head_dim ** (-0.5)
    block_count = lax.axis_size("ctx")
    gain_width = model_width // block_count
    block_index = lax.axis_index("ctx")
    first_row = block_index * row_count
    wa_index = lax.axis_index("wa")
    core = wa_index % CORES
    chip = wa_index // CORES
    half = row_count // CORES
    share = half // CHIPS
    own_start = core * half + chip * share
    reach_blocks = REACH // row_count
    bf16 = jnp.bfloat16

    def to_own_order(values):
        parts = values.reshape((CORES, CHIPS, share) + values.shape[1:])
        parts = rolled(rolled(parts, core, 0), chip, 1)
        return parts.reshape(values.shape)

    def to_token_order(values):
        parts = values.reshape((CORES, CHIPS, share) + values.shape[1:])
        parts = rolled(rolled(parts, (CORES - core) % CORES, 0), (CHIPS - chip) % CHIPS, 1)
        return parts.reshape(values.shape)

    def own_rows(values):
        return lax.dynamic_slice_in_dim(values, own_start, share, 0)

    def sum_own(partial):
        arrived = to_partner(partial[half:].astype(bf16))
        kept = partial[:half] + arrived.astype(jnp.float32)
        pieces = [
            along_z(kept[b * share : (b + 1) * share].astype(bf16), b) for b in range(1, CHIPS)
        ]
        total = kept[:share]
        for piece in pieces:
            total = total + piece.astype(jnp.float32)
        return total

    def sum_token_order(partial):
        sent = lax.dynamic_slice_in_dim(partial, (1 - core) * half, half, 0).astype(bf16)
        arrived = to_partner(sent)
        kept = lax.dynamic_slice_in_dim(partial, core * half, half, 0) + arrived.astype(jnp.float32)

        def piece_of(steps):
            return lax.dynamic_slice_in_dim(kept, ((chip + steps) % CHIPS) * share, share, 0)

        pieces = [along_z(piece_of(b).astype(bf16), b) for b in range(1, CHIPS)]
        total = piece_of(0)
        for piece in pieces:
            total = total + piece.astype(jnp.float32)
        return total

    def all_rows(owned):
        pieces = [owned] + [along_z(owned, CHIPS - b) for b in range(1, CHIPS)]
        mine = jnp.concatenate(pieces, axis=0)
        return jnp.concatenate([mine, to_partner(mine)], axis=0)

    def ffn_forward(hidden, gain_vec, gate_weight, lift_weight):
        normed, unit_rows, inverse = norm_forward(hidden, gain_vec)
        normed_rounded = all_rows(normed.astype(bf16))
        gate_values = jnp.dot(normed_rounded, gate_weight, preferred_element_type=jnp.float32)
        lift_values = jnp.dot(normed_rounded, lift_weight, preferred_element_type=jnp.float32)
        sigmoid_values = jax.nn.sigmoid(gate_values)
        activation = (gate_values * sigmoid_values * lift_values).astype(bf16)
        return (
            activation,
            (
                normed_rounded,
                unit_rows,
                inverse,
                gate_values,
                lift_values,
                sigmoid_values,
                activation,
            ),
        )

    def ffn_backward(
        grad_hidden, grad_rounded, saved, gain_vec, gate_weight, lift_weight, down_weight
    ):
        normed_rounded, unit_rows, inverse, gate_values, lift_values, sigmoid_values, activation = (
            saved
        )
        grad_activation = jnp.dot(grad_rounded, down_weight, preferred_element_type=jnp.float32)
        grad_gate = (
            grad_activation
            * lift_values
            * sigmoid_values
            * (1.0 + gate_values * (1.0 - sigmoid_values))
        ).astype(bf16)
        grad_lift = (grad_activation * gate_values * sigmoid_values).astype(bf16)
        grad_normed = sum_own(
            times_transposed(grad_gate, gate_weight) + times_transposed(grad_lift, lift_weight)
        )
        gate_grad = contract_rows(normed_rounded, grad_gate)
        lift_grad = contract_rows(normed_rounded, grad_lift)
        down_grad = contract_rows(grad_rounded, activation)
        gain_part = gain_total(grad_normed, unit_rows)
        grad_input = grad_hidden + norm_backward(grad_normed, unit_rows, inverse, gain_vec)
        return (grad_input, (gain_part, gate_grad, lift_grad, down_grad))

    edge_ids = jnp.full((2,), -1, jnp.int32)
    padded_ids = jnp.concatenate([edge_ids, segment_ids, edge_ids])
    window_ids = lax.dynamic_slice_in_dim(padded_ids, first_row, row_count + 4)
    own_ids = window_ids[2 : row_count + 2]
    back_one = (window_ids[1 : row_count + 1] == own_ids)[:, None]
    back_two = (window_ids[0:row_count] == own_ids)[:, None]
    ahead_one = (window_ids[3 : row_count + 3] == own_ids)[:, None]
    ahead_two = (window_ids[4 : row_count + 4] == own_ids)[:, None]

    base_hidden = tokens.astype(jnp.float32)
    mixer_normed, mixer_unit, mixer_inverse = norm_forward(base_hidden, mixnorm_gain)
    mixer_rounded = mixer_normed.astype(bf16)
    gate_before = jnp.dot(mixer_rounded, bgate_weight, preferred_element_type=jnp.float32)
    conv_value = jnp.dot(mixer_rounded, xvalue_weight, preferred_element_type=jnp.float32)
    conv_input = (gate_before * conv_value).astype(bf16)
    carried = passed_along(conv_input[row_count - 2 :], "ctx", 1)
    gate_after = jnp.dot(mixer_rounded, cgate_weight, preferred_element_type=jnp.float32)
    extended = jnp.concatenate([carried, conv_input], axis=0).astype(jnp.float32)
    conv_result = (
        conv_kernel[0] * extended[2:]
        + conv_kernel[1] * jnp.where(back_one, extended[1 : row_count + 1], 0.0)
        + conv_kernel[2] * jnp.where(back_two, extended[0:row_count], 0.0)
    )
    gated_rounded = (gate_after * conv_result).astype(bf16)
    own_tokens = own_rows(tokens).astype(jnp.float32)
    after_mixer = own_tokens + sum_token_order(times_transposed(gated_rounded, mixout_weight))

    lower_activation, lower_saved = ffn_forward(
        after_mixer, lowernorm_gain, lowergate_weight, lowerlift_weight
    )
    after_lower = after_mixer + sum_own(times_transposed(lower_activation, lowerdown_weight))

    attention_normed, attention_unit, attention_inverse = norm_forward(after_lower, attnnorm_gain)
    attention_rounded = all_rows(attention_normed.astype(bf16))
    query_raw = jnp.dot(
        attention_rounded, query_weight, preferred_element_type=jnp.float32
    ).reshape(row_count, 1, group_size, head_dim)
    keys_raw = jnp.dot(attention_rounded, key_weight, preferred_element_type=jnp.float32).reshape(
        row_count, 1, 1, head_dim
    )
    value_rows = jnp.dot(
        attention_rounded, value_weight, preferred_element_type=jnp.float32
    ).astype(bf16)
    query_normed, query_unit, query_inverse = norm_forward(query_raw, querynorm_gain)
    keys_normed, keys_unit, keys_inverse = norm_forward(keys_raw, keynorm_gain)
    cosine_table, sine_table = rope_tables(to_own_order(positions), head_dim)
    query_rotated = rotate(query_normed, cosine_table, sine_table).astype(bf16)
    keys_rotated = (
        rotate(keys_normed, cosine_table, sine_table).astype(bf16).reshape(row_count, head_dim)
    )

    own_pairs = jnp.concatenate([keys_rotated, value_rows], axis=1)
    arrived_pairs = lax.all_to_all(
        jnp.broadcast_to(own_pairs[None], (block_count,) + own_pairs.shape),
        "ctx",
        0,
        0,
        tiled=True,
    )
    pairs = lax.dynamic_slice_in_dim(
        jnp.concatenate(
            [jnp.zeros((reach_blocks,) + own_pairs.shape, bf16), arrived_pairs], axis=0
        ),
        block_index,
        reach_blocks + 1,
        0,
    ).reshape(-1, 2 * head_dim)
    key_heads = pairs[:, :head_dim]
    value_heads = pairs[:, head_dim:]
    block_starts = (
        first_row + row_count * (jnp.arange(reach_blocks + 1, dtype=jnp.int32) - reach_blocks)
    )
    id_window = lax.dynamic_slice_in_dim(
        jnp.concatenate([jnp.full((reach_blocks * row_count,), -1, jnp.int32), segment_ids]),
        first_row,
        (reach_blocks + 1) * row_count,
    ).reshape(reach_blocks + 1, row_count)
    row_order = to_own_order(jnp.arange(row_count, dtype=jnp.int32))
    query_index = first_row + row_order
    query_ids = to_own_order(own_ids)
    key_index = (block_starts[:, None] + row_order[None, :]).reshape(-1)
    key_ids = jax.vmap(to_own_order)(id_window).reshape(-1)
    allowed = (key_index[None, :] <= query_index[:, None]) & (key_ids[None, :] == query_ids[:, None])
    visible = allowed[:, None, :]
    query_heads = query_rotated.reshape(row_count, group_size, head_dim)
    scores = (
        jnp.einsum("tgd,sd->tgs", query_heads, key_heads, preferred_element_type=jnp.float32)
        * score_scale
    )
    scores = jnp.where(visible, scores, NEG_BIG)
    top_score = jnp.max(scores, axis=-1)
    weights = jnp.where(visible, jnp.exp(scores - top_score[..., None]), 0.0)
    total_weight = jnp.sum(weights, axis=-1)
    accumulated = jnp.einsum(
        "tgs,sd->tgd", weights.astype(bf16), value_heads, preferred_element_type=jnp.float32
    )
    mixed_heads = accumulated / total_weight[..., None]
    log_total = top_score + jnp.log(total_weight)
    mixed_rounded = mixed_heads.astype(bf16).reshape(row_count, group_size * head_dim)
    after_attention = after_lower + sum_own(times_transposed(mixed_rounded, attnout_weight))

    upper_activation, upper_saved = ffn_forward(
        after_attention, uppernorm_gain, uppergate_weight, upperlift_weight
    )
    own_order_cotangent = to_own_order(cotangent)
    grad_three, upper_terms = ffn_backward(
        own_rows(cotangent).astype(jnp.float32),
        own_order_cotangent,
        upper_saved,
        uppernorm_gain,
        uppergate_weight,
        upperlift_weight,
        upperdown_weight,
    )
    after_upper = after_attention + sum_own(times_transposed(upper_activation, upperdown_weight))
    block_output = to_token_order(all_rows(after_upper.astype(bf16)))

    three_rounded = all_rows(grad_three.astype(bf16))
    grad_mixed = jnp.dot(three_rounded, attnout_weight, preferred_element_type=jnp.float32)
    grad_heads = grad_mixed.astype(bf16).reshape(row_count, group_size, head_dim)
    delta_rows = jnp.sum(grad_heads.astype(jnp.float32) * mixed_heads, axis=-1)
    weights = jnp.where(visible, jnp.exp(scores - log_total[..., None]), 0.0)
    grad_weights = jnp.einsum(
        "tgd,sd->tgs", grad_heads, value_heads, preferred_element_type=jnp.float32
    )
    grad_scores = (weights * (grad_weights - delta_rows[..., None])).astype(bf16)
    query_back = (
        jnp.einsum("tgs,sd->tgd", grad_scores, key_heads, preferred_element_type=jnp.float32)
        * score_scale
    )
    key_part = (
        jnp.einsum("tgs,tgd->sd", grad_scores, query_heads, preferred_element_type=jnp.float32)
        * score_scale
    )
    value_part = jnp.einsum(
        "tgs,tgd->sd", weights.astype(bf16), grad_heads, preferred_element_type=jnp.float32
    )
    pair_parts = jnp.concatenate([key_part, value_part], axis=1).reshape(
        reach_blocks + 1, row_count, 2 * head_dim
    )
    pairs_back = pair_parts[reach_blocks]
    for k in range(1, reach_blocks + 1):
        pairs_back = pairs_back + passed_along(
            pair_parts[reach_blocks - k].astype(bf16), "ctx", -k
        ).astype(jnp.float32)
    keys_back = pairs_back[:, :head_dim]
    values_back = pairs_back[:, head_dim:]

    query_upstream = rotate_back(
        query_back.reshape(row_count, 1, group_size, head_dim), cosine_table, sine_table
    )
    keys_upstream = rotate_back(
        keys_back.reshape(row_count, 1, 1, head_dim), cosine_table, sine_table
    )
    querynorm_part = gain_total(query_upstream, query_unit)
    keynorm_part = gain_total(keys_upstream, keys_unit)
    grad_query = (
        norm_backward(query_upstream, query_unit, query_inverse, querynorm_gain)
        .astype(bf16)
        .reshape(row_count, group_size * head_dim)
    )
    grad_keys = (
        norm_backward(keys_upstream, keys_unit, keys_inverse, keynorm_gain)
        .astype(bf16)
        .reshape(row_count, head_dim)
    )
    grad_values = values_back.astype(bf16)
    grad_attention = sum_own(
        times_transposed(grad_query, query_weight)
        + times_transposed(grad_keys, key_weight)
        + times_transposed(grad_values, value_weight)
    )
    attnnorm_part = gain_total(grad_attention, attention_unit)
    grad_two = grad_three + norm_backward(
        grad_attention, attention_unit, attention_inverse, attnnorm_gain
    )
    grad_one, lower_terms = ffn_backward(
        grad_two,
        all_rows(grad_two.astype(bf16)),
        lower_saved,
        lowernorm_gain,
        lowergate_weight,
        lowerlift_weight,
        lowerdown_weight,
    )
    attention_grads = [
        contract_rows(attention_rounded, grad_query),
        contract_rows(attention_rounded, grad_keys),
        contract_rows(attention_rounded, grad_values),
        contract_rows(three_rounded, mixed_rounded),
    ]
    one_rounded = to_token_order(all_rows(grad_one.astype(bf16)))
    grad_gated = jnp.dot(one_rounded, mixout_weight, preferred_element_type=jnp.float32)
    grad_conv = grad_gated * gate_after
    following = passed_along(grad_conv[:2], "ctx", -1)
    grad_after_gate = (grad_gated * conv_result).astype(bf16)
    mixout_grad = contract_rows(one_rounded, gated_rounded)
    grad_extended = jnp.concatenate([grad_conv, following], axis=0)
    grad_conv_input = (
        conv_kernel[0] * grad_conv
        + conv_kernel[1] * jnp.where(ahead_one, grad_extended[1 : row_count + 1], 0.0)
        + conv_kernel[2] * jnp.where(ahead_two, grad_extended[2 : row_count + 2], 0.0)
    )
    kernel_local = jnp.stack(
        [
            jnp.sum(grad_conv * extended[2:], axis=0),
            jnp.sum(grad_conv * jnp.where(back_one, extended[1 : row_count + 1], 0.0), axis=0),
            jnp.sum(grad_conv * jnp.where(back_two, extended[0:row_count], 0.0), axis=0),
        ]
    )
    grad_before = (grad_conv_input * conv_value).astype(bf16)
    grad_value = (grad_conv_input * gate_before).astype(bf16)
    mixer_partial = (
        times_transposed(grad_before, bgate_weight)
        + times_transposed(grad_after_gate, cgate_weight)
        + times_transposed(grad_value, xvalue_weight)
    )
    grad_mixer = sum_token_order(mixer_partial)
    mixnorm_part = jnp.sum(mixer_partial * mixer_unit, axis=0)
    own_unit, own_inverse = (own_rows(mixer_unit), own_rows(mixer_inverse))
    own_tokens_grad = grad_one + norm_backward(grad_mixer, own_unit, own_inverse, mixnorm_gain)
    tokens_held = to_token_order(all_rows(own_tokens_grad.astype(bf16))).astype(jnp.float32)

    last_grads = jnp.concatenate(
        [
            contract_rows(mixer_rounded, grad_before),
            contract_rows(mixer_rounded, grad_after_gate),
            contract_rows(mixer_rounded, grad_value),
            mixout_grad,
        ],
        axis=1,
    ).astype(bf16)
    last_width = last_grads.shape[1]

    def by_block(vector):
        return vector.reshape(block_count, gain_width)

    def for_all(vector):
        return jnp.broadcast_to(vector.reshape(1, -1), (block_count, vector.size))

    small_parts = jnp.concatenate(
        [
            for_all(kernel_local),
            by_block(mixnorm_part),
            by_block(lower_terms[0]),
            by_block(attnnorm_part),
            by_block(upper_terms[0]),
            for_all(querynorm_part),
            for_all(keynorm_part),
        ],
        axis=1,
    ).astype(bf16)
    small_width = small_parts.shape[1]
    small_rows = -(-small_width // last_width)
    small_parts = jnp.pad(small_parts, ((0, 0), (0, small_rows * last_width - small_width)))
    outgoing = jnp.concatenate(
        [
            last_grads.reshape(block_count, gain_width, last_width),
            small_parts.reshape(block_count, small_rows, last_width),
        ],
        axis=1,
    )
    incoming = lax.all_to_all(outgoing, "ctx", 0, 0, tiled=True)
    last_sums = jnp.sum(incoming.astype(jnp.float32), axis=0)
    last_shares = last_sums[:gain_width]
    small_sums = last_sums[gain_width:].reshape(-1)[:small_width]
    kernel_grad = small_sums[: kernel_local.size].reshape(kernel_local.shape)
    gain_sums = small_sums[kernel_local.size :]
    gain_sums = gain_sums + to_partner(gain_sums)
    gain_pieces = [along_z(gain_sums, b) for b in range(1, CHIPS)]
    for piece in gain_pieces:
        gain_sums = gain_sums + piece
    gains = gain_sums.reshape(-1, gain_width)
    querynorm_grad = gain_sums[4 * gain_width : 4 * gain_width + head_dim]
    keynorm_grad = gain_sums[4 * gain_width + head_dim :]

    def scattered(parts):
        merged = lax.psum_scatter(
            jnp.concatenate([part.astype(bf16) for part in parts], axis=1).reshape(
                block_count, gain_width, -1
            ),
            "ctx",
            scatter_dimension=0,
            tiled=False,
        ).astype(jnp.float32)
        bounds = [0]
        for part in parts:
            bounds.append(bounds[-1] + part.shape[1])
        return [merged[:, low:high] for low, high in zip(bounds[:-1], bounds[1:])]

    upper_shares = scattered(list(upper_terms[1:]))
    lower_shares = scattered(list(lower_terms[1:]) + attention_grads)
    channels = bgate_weight.shape[1]
    return (
        block_output,
        tokens_held,
        gains[0],
        last_shares[:, :channels],
        last_shares[:, channels : 2 * channels],
        last_shares[:, 2 * channels : 3 * channels],
        kernel_grad,
        last_shares[:, 3 * channels :],
        gains[1],
        lower_shares[0],
        lower_shares[1],
        lower_shares[2],
        gains[2],
        lower_shares[3],
        lower_shares[4],
        lower_shares[5],
        querynorm_grad,
        keynorm_grad,
        lower_shares[6],
        gains[3],
        upper_shares[0],
        upper_shares[1],
        upper_shares[2],
    )


def solution(mesh):
    return jax.shard_map(
        shards,
        mesh=mesh,
        in_specs=(
            P("ctx", None),
            P(),
            P("ctx"),
            P(),
            P(None, "wa"),
            P(None, "wa"),
            P(None, "wa"),
            P(None, "wa"),
            P(None, "wa"),
            P(),
            P(None, "wa"),
            P(None, "wa"),
            P(None, "wa"),
            P(),
            P(None, "wa"),
            P(None, "wa"),
            P(None, "wa"),
            P(),
            P(),
            P(None, "wa"),
            P(),
            P(None, "wa"),
            P(None, "wa"),
            P(None, "wa"),
            P("ctx", None),
        ),
        out_specs=(
            P("ctx", None),
            P("ctx", None),
            P("ctx"),
            P("ctx", "wa"),
            P("ctx", "wa"),
            P("ctx", "wa"),
            P(None, "wa"),
            P("ctx", "wa"),
            P("ctx"),
            P("ctx", "wa"),
            P("ctx", "wa"),
            P("ctx", "wa"),
            P("ctx"),
            P("ctx", "wa"),
            P("ctx", "wa"),
            P("ctx", "wa"),
            P(),
            P(),
            P("ctx", "wa"),
            P("ctx"),
            P("ctx", "wa"),
            P("ctx", "wa"),
            P("ctx", "wa"),
        ),
        check_vma=False,
    )
```
